32 devices in a mesh: groups: 2 (over y), rows: 4 (over x, core), cents: 4 (over z).
Axes of the slice: x: 2, y: 2, z: 4, core: 2. Of those that a mesh axis runs over, the one named last changes fastest.
Arguments:
- embedding: bfloat16 [2048, 128], P(('groups', 'rows', 'cents')), parts along dimension 0, may hold values from -8 to 8
- degrees: int32 [2048], P(('groups', 'rows', 'cents')), parts along dimension 0, may hold values from 1 to 63
- rotation: float32 [128, 128], replicated, may hold values from -0.5 to 0.5
- offsets: float32 [8192, 128], P(('groups', 'cents')), parts along dimension 0, may hold values from -2 to 2
- seed_ids: int32 [8192], P(('groups', 'cents')), parts along dimension 0, may hold values from 0 to 1023
Outputs:
- energy: float32 [2048], P(('groups', 'rows', 'cents')), parts along dimension 0
- centroids: float32 [8192, 128], P(('groups', 'cents')), parts along dimension 0
The draws below stay inside these ranges and needn't reach their ends.
There are 2 independent parts, one for each index of `groups`. The reference program is written for one: setup_inputs(seed, part) draws one part's arguments, and reference() takes and returns one part's arrays. A program takes and returns all parts, laid end to end along the dimension named above; an argument that names none is the same for every part. Nothing has to cross between parts.
All inputs are finite; a program needn't handle non-finite values.
Results may differ from the reference program's by a relative error of at most 0.024.
Values may be sent and summed in bfloat16 or wider, within the bound.
A program may use at most 64 MiB of HBM per device.

```python
import jax
import jax.numpy as jnp
from jax import lax

K = 128
ITERS = 2
CENTROIDS = 4096
ROWS = 1024


def draw_embedding(key, part):
    first, second = jax.random.split(key, 2)
    scales = jnp.exp(jax.random.uniform(first, (K,), jnp.float32, jnp.log(0.3), jnp.log(3.0)))
    values = jax.random.normal(second, (ROWS, K), jnp.float32)
    return jnp.clip(values * scales[None, :], -8.0, 8.0).astype(jnp.bfloat16)


def draw_offsets(key, part):
    first = jax.random.fold_in(key, 0)
    return jnp.clip(0.05 * jax.random.normal(first, (CENTROIDS, K), jnp.float32), -2.0, 2.0)


def plant(values, key, smallest, high):
    longest = values.shape.index(max(values.shape))
    spots = []
    for shift in (0, 1):
        where = [jax.random.randint(jax.random.fold_in(key, axis), (), 0, length) for axis, length in enumerate(values.shape)]
        where[longest] = (where[longest] + shift) % values.shape[longest]
        spots.append(tuple(where))
    return values.at[spots[0]].set(smallest).at[spots[1]].set(high)


def gaussian(own_key, shape, scale, most, held_as=jnp.bfloat16):
    values = jax.random.normal(own_key, shape, jnp.float32) * scale
    return jnp.minimum(jnp.maximum(values, -most), most).astype(held_as)


def setup_inputs(seed: int = 0, part: int = 0) -> dict:
    arg_keys = jax.random.split(jax.random.key(seed), 6)
    part_splits = jax.random.split(jax.random.fold_in(arg_keys[5], part), 6)
    embedding = draw_embedding(jax.random.fold_in(jax.random.fold_in(arg_keys[5], part), 71), part)
    degrees = plant(jax.random.randint(part_splits[1], (ROWS,), 1, 64), jax.random.fold_in(part_splits[1], 1), 1, 63).astype(jnp.int32)
    rotation = gaussian(arg_keys[2], (K, K), K ** -0.5, 0.5, jnp.float32)
    offsets = draw_offsets(jax.random.fold_in(jax.random.fold_in(arg_keys[5], part), 71), part)
    seed_ids = plant(jax.random.randint(part_splits[4], (CENTROIDS,), 0, ROWS), jax.random.fold_in(part_splits[4], 1), 0, ROWS - 1).astype(jnp.int32)
    return dict(embedding=embedding, degrees=degrees, rotation=rotation, offsets=offsets, seed_ids=seed_ids)


sharpness_scale = 0.1
ridge = 0.01

def lower_factor(matrix):
    width = matrix.shape[0]
    positions = jnp.arange(width, dtype=jnp.int32)

    def column_step(index, factor):
        row_here = lax.dynamic_index_in_dim(factor, index, 0, keepdims=False)
        column = lax.dynamic_index_in_dim(matrix, index, 1, keepdims=False)
        column = column - jnp.dot(factor, row_here, precision=lax.Precision.HIGHEST)
        pivot = jnp.sqrt(lax.dynamic_index_in_dim(column, index, 0, keepdims=False))
        column = jnp.where(positions > index, column / pivot, jnp.zeros((), column.dtype))
        column = jnp.where(positions == index, pivot, column)
        return lax.dynamic_update_slice_in_dim(factor, column[:, None], index, 1)
    return lax.fori_loop(0, width, column_step, jnp.zeros(matrix.shape, matrix.dtype))

def upper_solve(factor, target):
    width = factor.shape[0]

    def row_step(count, solved):
        index = width - 1 - count
        column = lax.dynamic_index_in_dim(factor, index, 1, keepdims=False)
        pivot = lax.dynamic_index_in_dim(column, index, 0, keepdims=False)
        target_row = lax.dynamic_index_in_dim(target, index, 0, keepdims=False)
        value = (target_row - jnp.dot(column, solved, precision=lax.Precision.HIGHEST)) / pivot
        return lax.dynamic_update_slice_in_dim(solved, value[None, :], index, 0)
    return lax.fori_loop(0, width, row_step, jnp.zeros(target.shape, target.dtype))

def block_affinity_logits(rows_block, piece_entry_lengths, cent_bf, mean_point_sqlength):
    pairwise_dots = lax.dot_general(rows_block, cent_bf, (((1,), (1,)), ((), ())), preferred_element_type=jnp.float32)
    return (2.0 * pairwise_dots - mean_point_sqlength[None, :] - piece_entry_lengths[:, None]) / sharpness_scale

def reference(embedding, degrees, rotation, offsets, seed_ids):
    total_rows = embedding.shape[0]
    width = embedding.shape[1]
    gram = lax.dot_general(embedding, embedding, (((0,), (0,)), ((), ())), preferred_element_type=jnp.float32)
    shifted = gram / total_rows + ridge * jnp.eye(width, dtype=jnp.float32)
    cholesky_lower_factor = lower_factor(shifted)
    turned = upper_solve(cholesky_lower_factor, rotation).astype(jnp.bfloat16)
    mixed = jnp.dot(embedding, turned, preferred_element_type=jnp.float32)
    unit = (mixed * lax.rsqrt(lax.optimization_barrier(jnp.sum(mixed * mixed, axis=1, keepdims=True)) + 1e-06)).astype(jnp.bfloat16)
    weights = jnp.sqrt(degrees.astype(jnp.float32))
    sq_norms = lax.optimization_barrier(jnp.sum(jnp.square(unit.astype(jnp.float32)), axis=1))
    centers = jnp.take(unit, seed_ids.astype(jnp.int32), axis=0).astype(jnp.float32) + offsets
    block_rows = min(512, total_rows)
    block_count = total_rows // block_rows
    rows_blocks = unit.reshape(block_count, block_rows, width)
    norm_blocks = sq_norms.reshape(block_count, block_rows)
    weight_blocks = weights.reshape(block_count, block_rows)
    energy = jnp.zeros((total_rows,), jnp.float32)
    for step in range(ITERS):
        cent_bf = centers.astype(jnp.bfloat16)
        mean_point_sqlength = lax.optimization_barrier(jnp.sum(centers * centers, axis=1))

        def accumulate(carry, pack):
            logits = block_affinity_logits(pack[0], pack[1], cent_bf, mean_point_sqlength)
            top = lax.optimization_barrier(jnp.max(logits, axis=1))
            expd = jnp.exp(logits - top[:, None])
            total = lax.optimization_barrier(jnp.sum(expd, axis=1))
            shares = (pack[2][:, None] * (expd / total[:, None])).astype(jnp.bfloat16)
            moved = lax.dot_general(shares, pack[0], (((0,), (0,)), ((), ())), preferred_element_type=jnp.float32)
            new_carry = (carry[0] + moved, carry[1] + lax.optimization_barrier(jnp.sum(shares.astype(jnp.float32), axis=0)))
            return (new_carry, top + jnp.log(total))
        start = (jnp.zeros(centers.shape, jnp.float32), jnp.zeros((centers.shape[0],), jnp.float32))
        (sums, masses), energies = lax.scan(accumulate, start, (rows_blocks, norm_blocks, weight_blocks))
        energy = energies.reshape(total_rows)
        centers = (sums + centers) / (masses + 1.0)[:, None]
    return (energy, centers)
```

```python
import functools
import math

import jax
import jax.numpy as jnp
from jax import lax
from jax.experimental import pallas as pl
from jax.experimental.pallas import tpu as pltpu
from jax.sharding import PartitionSpec as P

ITERS = 2


sharpness_scale = 0.1
ridge = 0.01


def lower_factor(matrix):
    width = matrix.shape[0]
    positions = jnp.arange(width, dtype=jnp.int32)

    def column_step(index, factor):
        row_here = lax.dynamic_index_in_dim(factor, index, 0, keepdims=False)
        column = lax.dynamic_index_in_dim(matrix, index, 1, keepdims=False)
        column = column - jnp.dot(factor, row_here, precision=lax.Precision.HIGHEST)
        pivot = jnp.sqrt(lax.dynamic_index_in_dim(column, index, 0, keepdims=False))
        column = jnp.where(positions > index, column / pivot, jnp.zeros((), column.dtype))
        column = jnp.where(positions == index, pivot, column)
        return lax.dynamic_update_slice_in_dim(factor, column[:, None], index, 1)

    return lax.fori_loop(0, width, column_step, jnp.zeros(matrix.shape, matrix.dtype))


def upper_solve(factor, target):
    width = factor.shape[0]

    def row_step(count, solved):
        index = width - 1 - count
        column = lax.dynamic_index_in_dim(factor, index, 1, keepdims=False)
        pivot = lax.dynamic_index_in_dim(column, index, 0, keepdims=False)
        target_row = lax.dynamic_index_in_dim(target, index, 0, keepdims=False)
        value = (target_row - jnp.dot(column, solved, precision=lax.Precision.HIGHEST)) / pivot
        return lax.dynamic_update_slice_in_dim(solved, value[None, :], index, 0)

    return lax.fori_loop(0, width, row_step, jnp.zeros(target.shape, target.dtype))


def block_affinity_logits(rows_block, piece_entry_lengths, cent_bf, mean_point_sqlength):
    pairwise_dots = lax.dot_general(
        rows_block, cent_bf, (((1,), (1,)), ((), ())), preferred_element_type=jnp.float32
    )
    return (
        2.0 * pairwise_dots - mean_point_sqlength[None, :] - piece_entry_lengths[:, None]
    ) / sharpness_scale


def shards(embedding, degrees, rotation, offsets, seed_ids):
    local_entries = embedding.shape[0]
    width = embedding.shape[1]
    total_rows = local_entries * lax.axis_size("rows") * lax.axis_size("cents")
    partial_gram_matrix = lax.dot_general(
        embedding, embedding, (((0,), (0,)), ((), ())), preferred_element_type=jnp.float32
    )
    gram = lax.psum(partial_gram_matrix, ("rows", "cents"))
    shifted = gram / total_rows + ridge * jnp.eye(width, dtype=jnp.float32)
    cholesky_lower_factor = lower_factor(shifted)
    turned = upper_solve(cholesky_lower_factor, rotation).astype(jnp.bfloat16)
    mixed = jnp.dot(embedding, turned, preferred_element_type=jnp.float32)
    unit = (mixed * lax.rsqrt(jnp.sum(mixed * mixed, axis=1, keepdims=True) + 1e-06)).astype(
        jnp.bfloat16
    )
    gathered, degree_rows = (
        lax.all_gather(unit, "cents", axis=0, tiled=True),
        lax.all_gather(degrees.astype(jnp.bfloat16), "cents", axis=0, tiled=True),
    )
    count = gathered.shape[0]
    weights = jnp.sqrt(degree_rows.astype(jnp.float32))
    sq_norms = jnp.sum(jnp.square(gathered.astype(jnp.float32)), axis=1)
    local_ids = seed_ids - lax.axis_index("rows") * count
    block_rows = min(512, count)
    block_count = count // block_rows
    rows_blocks = gathered.reshape(block_count, block_rows, width)
    norm_blocks = sq_norms.reshape(block_count, block_rows)
    weight_blocks = weights.reshape(block_count, block_rows)
    block_starts = jnp.arange(block_count, dtype=jnp.int32) * block_rows
    row_positions = jnp.arange(block_rows, dtype=jnp.int32)

    def seed_block(carry, pack):
        selector = ((local_ids - pack[1])[:, None] == row_positions[None, :]).astype(jnp.bfloat16)
        return (carry + jnp.dot(selector, pack[0], preferred_element_type=jnp.float32), None)

    picked_sum, unused_seed = lax.scan(
        seed_block, jnp.zeros((seed_ids.shape[0], width), jnp.float32), (rows_blocks, block_starts)
    )
    picked = picked_sum.astype(jnp.bfloat16)
    centers = lax.psum(picked, "rows").astype(jnp.float32) + offsets
    energy = jnp.zeros((count,), jnp.float32)
    for step in range(ITERS):
        cent_bf = centers.astype(jnp.bfloat16)
        mean_point_sqlength = jnp.sum(centers * centers, axis=1)

        def local_stats(pack):
            logits = block_affinity_logits(pack[0], pack[1], cent_bf, mean_point_sqlength)
            peak = jnp.max(logits, axis=1)
            return (peak, jnp.sum(jnp.exp(logits - peak[:, None]), axis=1))

        peaks, totals = lax.map(local_stats, (rows_blocks, norm_blocks))
        larger = lax.pmax(peaks, "cents")
        whole = lax.psum(totals * jnp.exp(peaks - larger), "cents")

        def accumulate(carry, pack):
            logits = block_affinity_logits(pack[0], pack[1], cent_bf, mean_point_sqlength)
            probs = jnp.exp(logits - pack[2][:, None]) / pack[3][:, None]
            shares = (pack[4][:, None] * probs).astype(jnp.bfloat16)
            moved = lax.dot_general(
                shares, pack[0], (((0,), (0,)), ((), ())), preferred_element_type=jnp.float32
            )
            return (
                (carry[0] + moved, carry[1] + jnp.sum(shares.astype(jnp.float32), axis=0)),
                None,
            )

        start = (jnp.zeros(centers.shape, jnp.float32), jnp.zeros((centers.shape[0],), jnp.float32))
        (sums, masses), unused = lax.scan(
            accumulate, start, (rows_blocks, norm_blocks, larger, whole, weight_blocks)
        )
        energy = (larger + jnp.log(whole)).reshape(count)
        full_sums, full_masses = (
            lax.psum(sums.astype(jnp.bfloat16), "rows").astype(jnp.float32),
            lax.psum(masses.astype(jnp.bfloat16), "rows").astype(jnp.float32),
        )
        centers = (full_sums + centers) / (full_masses + 1.0)[:, None]
    own_energy = lax.dynamic_slice_in_dim(
        energy, lax.axis_index("cents") * local_entries, local_entries
    )
    return (own_energy, centers)


MESH = pl.DeviceIdType.MESH
LOG2E = math.log2(math.e)
LN2 = math.log(2.0)
GATHER_ROWS = 2048
BLOCK = 8


def vmem(count):
    return [pl.BlockSpec(memory_space=pltpu.VMEM)] * count


def gather_kernel(n_rows, n_cents, emb_ref, deg_ref, all_ref, weight_ref, shifted_ref, held, send_sem, recv_sem):
    group = lax.axis_index("groups")
    me = lax.axis_index("rows") * n_cents + lax.axis_index("cents")
    members = n_rows * n_cents
    local, width = emb_ref.shape

    def peer(step):
        other = lax.rem(me + step, members)
        return (group, other // n_cents, lax.rem(other, n_cents))

    barrier = pltpu.get_barrier_semaphore()
    for step in range(1, members):
        pl.semaphore_signal(barrier, inc=1, device_id=peer(step), device_id_type=MESH)
    held[me, :local, :] = emb_ref[...]
    tag = jnp.concatenate(
        [deg_ref[...].astype(jnp.float32), jnp.zeros((1, width - local), jnp.float32)], axis=1
    )
    held[me, local:, :] = jnp.broadcast_to(tag, (16, width)).astype(jnp.bfloat16)
    pl.semaphore_wait(barrier, members - 1)
    copies = []
    for step in range(1, members):
        copy = pltpu.make_async_remote_copy(
            src_ref=held.at[me],
            dst_ref=held.at[me],
            send_sem=send_sem.at[step - 1],
            recv_sem=recv_sem.at[step - 1],
            device_id=peer(step),
            device_id_type=MESH,
        )
        copy.start()
        copies.append(copy)
    for copy in copies:
        copy.wait()
    rows = held[:, :local, :].reshape(members * local, width)
    all_ref[...] = rows
    gram = lax.dot_general(rows, rows, (((0,), (0,)), ((), ())), preferred_element_type=jnp.float32)
    eye = lax.broadcasted_iota(jnp.int32, gram.shape, 0) == lax.broadcasted_iota(jnp.int32, gram.shape, 1)
    shifted_ref[...] = gram / (members * local) + jnp.where(eye, ridge, 0.0)
    tags = held[:, local:, :].astype(jnp.float32)
    weight_ref[...] = jnp.sqrt(
        jnp.concatenate([tags[index, :1, :local] for index in range(members)], axis=1)
    )


def factor_kernel(matrix_ref, rotation_ref, turned_ref):
    width = matrix_ref.shape[0]
    left = matrix_ref[...]
    row_id = lax.broadcasted_iota(jnp.int32, (width, width), 0)
    col_id = lax.broadcasted_iota(jnp.int32, (width, width), 1)
    right = jnp.where(row_id == col_id, 1.0, 0.0).astype(jnp.float32)
    both = jnp.concatenate([left, right], axis=1)
    sub = lax.broadcasted_iota(jnp.int32, (BLOCK, width), 0)
    solved = []
    for block in range(width // BLOCK):
        at = block * BLOCK
        a = both[at : at + BLOCK, :width]
        v = both[at : at + BLOCK, width:]
        columns = [jnp.broadcast_to(a[:, at + j : at + j + 1], (BLOCK, width)) for j in range(BLOCK)]
        pivots = jnp.ones((BLOCK, width), jnp.float32)
        for j in range(BLOCK):
            pivot = columns[j][j : j + 1, :]
            inverse = 1.0 / pivot
            pivots = jnp.where(sub == j, pivot, pivots)
            share = jnp.where(sub > j, columns[j] * inverse, 0.0)
            for l in range(j + 1, BLOCK):
                columns[l] = columns[l] - share * columns[l][j : j + 1, :]
            a = a - share * a[j : j + 1, :]
            v = v - share * v[j : j + 1, :]
        solved.append(v * lax.rsqrt(pivots))
        if at + BLOCK < width:
            both = both - lax.dot_general(
                a / pivots,
                jnp.concatenate([a, v], axis=1),
                (((0,), (0,)), ((), ())),
                preferred_element_type=jnp.float32,
                precision=lax.Precision.HIGHEST,
            )
    inverse_factor = jnp.concatenate(solved, axis=0)
    turned_ref[...] = lax.dot_general(
        inverse_factor,
        rotation_ref[...],
        (((0,), (0,)), ((), ())),
        preferred_element_type=jnp.float32,
        precision=lax.Precision.HIGHEST,
    ).astype(jnp.bfloat16)


def cluster_kernel(
    n_cents, local, all_ref, turned_ref, weight_ref, seed_ref, offset_ref, energy_ref, center_ref,
    pick, scores, probs, across, mine, theirs, send_sem, recv_sem,
):
    group, row = lax.axis_index("groups"), lax.axis_index("rows")
    me = lax.axis_index("cents")
    total_rows, width = all_ref.shape
    count = center_ref.shape[0]
    chunk = 128

    def peer(step):
        return (group, row, lax.rem(me + step, n_cents))

    barrier = pltpu.get_barrier_semaphore()
    for step in range(1, n_cents):
        pl.semaphore_signal(barrier, inc=1, device_id=peer(step), device_id_type=MESH)

    for at in range(0, total_rows, chunk):
        ids = lax.broadcasted_iota(jnp.int32, (chunk, count), 0) + at
        pick[at : at + chunk, :] = jnp.where(ids == seed_ref[...], 1.0, 0.0).astype(jnp.bfloat16)

    mixed = jnp.dot(all_ref[...], turned_ref[...], preferred_element_type=jnp.float32)
    length = jnp.sum(mixed * mixed, axis=1, keepdims=True)
    unit = (mixed * lax.rsqrt(length + 1e-06)).astype(jnp.bfloat16)
    turned_unit = unit.astype(jnp.float32).T
    norm = jnp.sum(turned_unit * turned_unit, axis=0, keepdims=True)
    across[...] = turned_unit.astype(jnp.bfloat16)
    picked = jnp.dot(across[...], pick[...], preferred_element_type=jnp.float32)
    center_ref[...] = picked.T + offset_ref[...]
    pl.semaphore_wait(barrier, n_cents - 1)

    scale = LOG2E / sharpness_scale
    for turn in range(ITERS):
        peak8 = jnp.full((8, total_rows), -jnp.inf, jnp.float32)
        for at in range(0, count, chunk):
            center = center_ref[at : at + chunk, :]
            square = jnp.sum(center * center, axis=1, keepdims=True) * scale
            dots = jnp.dot(center.astype(jnp.bfloat16), across[...], preferred_element_type=jnp.float32)
            score = dots * (2.0 * scale) - square
            scores[at : at + chunk, :] = score
            peak8 = jnp.maximum(peak8, jnp.max(score.reshape(chunk // 8, 8, total_rows), axis=0))
        peak = jnp.max(peak8, axis=0, keepdims=True)
        total8 = jnp.zeros((8, total_rows), jnp.float32)
        for at in range(0, count, chunk):
            prob = jnp.exp2(scores[at : at + chunk, :] - peak)
            probs[at : at + chunk, :] = prob.astype(jnp.bfloat16)
            total8 = total8 + jnp.sum(prob.reshape(chunk // 8, 8, total_rows), axis=0)
        total = jnp.sum(total8, axis=0, keepdims=True)
        mine[turn, 0:1, :] = peak
        mine[turn, 1:2, :] = total
        copies = []
        for step in range(1, n_cents):
            copy = pltpu.make_async_remote_copy(
                src_ref=mine.at[turn],
                dst_ref=theirs.at[turn, step - 1],
                send_sem=send_sem.at[turn, step - 1],
                recv_sem=recv_sem.at[turn, step - 1],
                device_id=peer(step),
                device_id_type=MESH,
            )
            copy.start()
            copies.append(copy)
        for copy in copies:
            copy.wait()
        top = peak
        for step in range(1, n_cents):
            top = jnp.maximum(top, theirs[turn, step - 1, 0:1, :])
        own = jnp.exp2(peak - top)
        whole = total * own
        for step in range(1, n_cents):
            whole = whole + theirs[turn, step - 1, 1:2, :] * jnp.exp2(theirs[turn, step - 1, 0:1, :] - top)
        share = weight_ref[...] * own / whole
        high = share.astype(jnp.bfloat16).astype(jnp.float32)
        sub = lax.broadcasted_iota(jnp.int32, (16, total_rows), 0)
        tail = jnp.where(sub == 0, high, jnp.where(sub == 1, share - high, 0.0)).astype(jnp.bfloat16)
        moved = jnp.concatenate(
            [
                (across[...].astype(jnp.float32) * share).astype(jnp.bfloat16),
                tail,
                jnp.zeros((width - 16, total_rows), jnp.bfloat16),
            ],
            axis=0,
        )
        for at in range(0, count, 256):
            sums = lax.dot_general(
                probs[at : at + 256, :], moved, (((1,), (1,)), ((), ())), preferred_element_type=jnp.float32
            )
            mass = sums[:, width : width + 1] + sums[:, width + 1 : width + 2]
            center_ref[at : at + 256, :] = (sums[:, :width] + center_ref[at : at + 256, :]) / (mass + 1.0)
        if turn == ITERS - 1:
            energy = top * LN2 + jnp.log(whole) - norm / sharpness_scale
            index = row * n_cents + me
            kept = jnp.zeros((1, local), jnp.float32)
            for place in range(total_rows // local):
                kept = jnp.where(index == place, energy[:, place * local : (place + 1) * local], kept)
            energy_ref[...] = kept


def gathered_shards(n_rows, n_cents, embedding, degrees, rotation, offsets, seed_ids):
    local, width = embedding.shape
    members = n_rows * n_cents
    total_rows = local * members
    count = offsets.shape[0]
    everyone, weight, shifted = pl.pallas_call(
        functools.partial(gather_kernel, n_rows, n_cents),
        out_shape=(
            jax.ShapeDtypeStruct((total_rows, width), jnp.bfloat16),
            jax.ShapeDtypeStruct((1, total_rows), jnp.float32),
            jax.ShapeDtypeStruct((width, width), jnp.float32),
        ),
        in_specs=vmem(2),
        out_specs=tuple(vmem(3)),
        scratch_shapes=[
            pltpu.VMEM((members, local + 16, width), jnp.bfloat16),
            pltpu.SemaphoreType.DMA((members - 1,)),
            pltpu.SemaphoreType.DMA((members - 1,)),
        ],
        compiler_params=pltpu.CompilerParams(collective_id=0, has_side_effects=True),
    )(embedding, degrees.reshape(1, local))
    turned = pl.pallas_call(
        factor_kernel,
        out_shape=jax.ShapeDtypeStruct((width, width), jnp.bfloat16),
        in_specs=vmem(2),
        out_specs=vmem(1)[0],
    )(shifted, rotation)
    energy, centers = pl.pallas_call(
        functools.partial(cluster_kernel, n_cents, local),
        out_shape=(
            jax.ShapeDtypeStruct((1, local), jnp.float32),
            jax.ShapeDtypeStruct((count, width), jnp.float32),
        ),
        in_specs=vmem(5),
        out_specs=tuple(vmem(2)),
        scratch_shapes=[
            pltpu.VMEM((total_rows, count), jnp.bfloat16),
            pltpu.VMEM((count, total_rows), jnp.float32),
            pltpu.VMEM((count, total_rows), jnp.bfloat16),
            pltpu.VMEM((width, total_rows), jnp.bfloat16),
            pltpu.VMEM((ITERS, 2, total_rows), jnp.float32),
            pltpu.VMEM((ITERS, n_cents - 1, 2, total_rows), jnp.float32),
            pltpu.SemaphoreType.DMA((ITERS, n_cents - 1)),
            pltpu.SemaphoreType.DMA((ITERS, n_cents - 1)),
        ],
        compiler_params=pltpu.CompilerParams(
            collective_id=1, has_side_effects=True, vmem_limit_bytes=40 * 1024 * 1024
        ),
    )(everyone, turned, weight, seed_ids.reshape(1, count), offsets)
    return energy.reshape(local), centers


def solution(mesh):
    n_rows, n_cents = mesh.shape["rows"], mesh.shape["cents"]

    def program(embedding, degrees, rotation, offsets, seed_ids):
        if embedding.shape[0] * n_rows * n_cents <= GATHER_ROWS:
            return gathered_shards(n_rows, n_cents, embedding, degrees, rotation, offsets, seed_ids)
        return shards(embedding, degrees, rotation, offsets, seed_ids)

    placed = (
        P(("groups", "rows", "cents"), None),
        P(("groups", "rows", "cents")),
        P(),
        P(("groups", "cents"), None),
        P(("groups", "cents")),
    )
    return jax.shard_map(
        program,
        mesh=mesh,
        in_specs=placed,
        out_specs=(P(("groups", "rows", "cents")), P(("groups", "cents"), None)),
        check_vma=False,
    )
```

```python
import functools
import math

import jax
import jax.numpy as jnp
from jax import lax
from jax.experimental import pallas as pl
from jax.experimental.pallas import tpu as pltpu
from jax.sharding import PartitionSpec as P

ITERS = 2


sharpness_scale = 0.1
ridge = 0.01


def lower_factor(matrix):
    width = matrix.shape[0]
    positions = jnp.arange(width, dtype=jnp.int32)

    def column_step(index, factor):
        row_here = lax.dynamic_index_in_dim(factor, index, 0, keepdims=False)
        column = lax.dynamic_index_in_dim(matrix, index, 1, keepdims=False)
        column = column - jnp.dot(factor, row_here, precision=lax.Precision.HIGHEST)
        pivot = jnp.sqrt(lax.dynamic_index_in_dim(column, index, 0, keepdims=False))
        column = jnp.where(positions > index, column / pivot, jnp.zeros((), column.dtype))
        column = jnp.where(positions == index, pivot, column)
        return lax.dynamic_update_slice_in_dim(factor, column[:, None], index, 1)

    return lax.fori_loop(0, width, column_step, jnp.zeros(matrix.shape, matrix.dtype))


def upper_solve(factor, target):
    width = factor.shape[0]

    def row_step(count, solved):
        index = width - 1 - count
        column = lax.dynamic_index_in_dim(factor, index, 1, keepdims=False)
        pivot = lax.dynamic_index_in_dim(column, index, 0, keepdims=False)
        target_row = lax.dynamic_index_in_dim(target, index, 0, keepdims=False)
        value = (target_row - jnp.dot(column, solved, precision=lax.Precision.HIGHEST)) / pivot
        return lax.dynamic_update_slice_in_dim(solved, value[None, :], index, 0)

    return lax.fori_loop(0, width, row_step, jnp.zeros(target.shape, target.dtype))


def block_affinity_logits(rows_block, piece_entry_lengths, cent_bf, mean_point_sqlength):
    pairwise_dots = lax.dot_general(
        rows_block, cent_bf, (((1,), (1,)), ((), ())), preferred_element_type=jnp.float32
    )
    return (
        2.0 * pairwise_dots - mean_point_sqlength[None, :] - piece_entry_lengths[:, None]
    ) / sharpness_scale


def shards(embedding, degrees, rotation, offsets, seed_ids):
    local_entries = embedding.shape[0]
    width = embedding.shape[1]
    total_rows = local_entries * lax.axis_size("rows") * lax.axis_size("cents")
    partial_gram_matrix = lax.dot_general(
        embedding, embedding, (((0,), (0,)), ((), ())), preferred_element_type=jnp.float32
    )
    gram = lax.psum(partial_gram_matrix, ("rows", "cents"))
    shifted = gram / total_rows + ridge * jnp.eye(width, dtype=jnp.float32)
    cholesky_lower_factor = lower_factor(shifted)
    turned = upper_solve(cholesky_lower_factor, rotation).astype(jnp.bfloat16)
    mixed = jnp.dot(embedding, turned, preferred_element_type=jnp.float32)
    unit = (mixed * lax.rsqrt(jnp.sum(mixed * mixed, axis=1, keepdims=True) + 1e-06)).astype(
        jnp.bfloat16
    )
    gathered, degree_rows = (
        lax.all_gather(unit, "cents", axis=0, tiled=True),
        lax.all_gather(degrees.astype(jnp.bfloat16), "cents", axis=0, tiled=True),
    )
    count = gathered.shape[0]
    weights = jnp.sqrt(degree_rows.astype(jnp.float32))
    sq_norms = jnp.sum(jnp.square(gathered.astype(jnp.float32)), axis=1)
    local_ids = seed_ids - lax.axis_index("rows") * count
    block_rows = min(512, count)
    block_count = count // block_rows
    rows_blocks = gathered.reshape(block_count, block_rows, width)
    norm_blocks = sq_norms.reshape(block_count, block_rows)
    weight_blocks = weights.reshape(block_count, block_rows)
    block_starts = jnp.arange(block_count, dtype=jnp.int32) * block_rows
    row_positions = jnp.arange(block_rows, dtype=jnp.int32)

    def seed_block(carry, pack):
        selector = ((local_ids - pack[1])[:, None] == row_positions[None, :]).astype(jnp.bfloat16)
        return (carry + jnp.dot(selector, pack[0], preferred_element_type=jnp.float32), None)

    picked_sum, unused_seed = lax.scan(
        seed_block, jnp.zeros((seed_ids.shape[0], width), jnp.float32), (rows_blocks, block_starts)
    )
    picked = picked_sum.astype(jnp.bfloat16)
    centers = lax.psum(picked, "rows").astype(jnp.float32) + offsets
    energy = jnp.zeros((count,), jnp.float32)
    for step in range(ITERS):
        cent_bf = centers.astype(jnp.bfloat16)
        mean_point_sqlength = jnp.sum(centers * centers, axis=1)

        def local_stats(pack):
            logits = block_affinity_logits(pack[0], pack[1], cent_bf, mean_point_sqlength)
            peak = jnp.max(logits, axis=1)
            return (peak, jnp.sum(jnp.exp(logits - peak[:, None]), axis=1))

        peaks, totals = lax.map(local_stats, (rows_blocks, norm_blocks))
        larger = lax.pmax(peaks, "cents")
        whole = lax.psum(totals * jnp.exp(peaks - larger), "cents")

        def accumulate(carry, pack):
            logits = block_affinity_logits(pack[0], pack[1], cent_bf, mean_point_sqlength)
            probs = jnp.exp(logits - pack[2][:, None]) / pack[3][:, None]
            shares = (pack[4][:, None] * probs).astype(jnp.bfloat16)
            moved = lax.dot_general(
                shares, pack[0], (((0,), (0,)), ((), ())), preferred_element_type=jnp.float32
            )
            return (
                (carry[0] + moved, carry[1] + jnp.sum(shares.astype(jnp.float32), axis=0)),
                None,
            )

        start = (jnp.zeros(centers.shape, jnp.float32), jnp.zeros((centers.shape[0],), jnp.float32))
        (sums, masses), unused = lax.scan(
            accumulate, start, (rows_blocks, norm_blocks, larger, whole, weight_blocks)
        )
        energy = (larger + jnp.log(whole)).reshape(count)
        full_sums, full_masses = (
            lax.psum(sums.astype(jnp.bfloat16), "rows").astype(jnp.float32),
            lax.psum(masses.astype(jnp.bfloat16), "rows").astype(jnp.float32),
        )
        centers = (full_sums + centers) / (full_masses + 1.0)[:, None]
    own_energy = lax.dynamic_slice_in_dim(
        energy, lax.axis_index("cents") * local_entries, local_entries
    )
    return (own_energy, centers)


MESH = pl.DeviceIdType.MESH
LOG2E = math.log2(math.e)
LN2 = math.log(2.0)
VMEM_LIMIT = 56 * 1024 * 1024
BLOCK = 32


def inverse_factor(matrix):
    width = matrix.shape[0]
    row_id = lax.broadcasted_iota(jnp.int32, (width, width), 0)
    col_id = lax.broadcasted_iota(jnp.int32, (width, width), 1)
    left = matrix
    right = jnp.where(row_id == col_id, 1.0, 0.0).astype(jnp.float32)
    sub = lax.broadcasted_iota(jnp.int32, (BLOCK, width), 0)
    solved = []
    for at in range(0, width, BLOCK):
        a, v = left[:BLOCK], right[:BLOCK]
        columns = [jnp.broadcast_to(a[:, at + j : at + j + 1], (BLOCK, width)) for j in range(BLOCK)]
        pivots = jnp.ones((BLOCK, width), jnp.float32)
        for j in range(BLOCK):
            low = j // 8 * 8

            def lower(old, new):
                return new if low == 0 else jnp.concatenate([old[:low], new], axis=0)

            pivot = columns[j][j : j + 1, :]
            pivots = jnp.where(sub == j, pivot, pivots)
            share = jnp.where(sub[low:] > j, columns[j][low:] * (1.0 / pivot), 0.0)
            for l in range(j + 1, BLOCK):
                columns[l] = lower(columns[l], columns[l][low:] - share * columns[l][j : j + 1, :])
            a = lower(a, a[low:] - share * a[j : j + 1, :])
            v = lower(v, v[low:] - share * v[j : j + 1, :])
        solved.append(v * lax.rsqrt(pivots))
        if at + BLOCK < width:
            update = lax.dot_general(
                a / pivots,
                jnp.concatenate([a, v], axis=1),
                (((0,), (0,)), ((), ())),
                preferred_element_type=jnp.float32,
                precision=lax.Precision.HIGHEST,
            )[at + BLOCK :]
            left = left[BLOCK:] - update[:, :width]
            right = right[BLOCK:] - update[:, width:]
    return jnp.concatenate(solved, axis=0)


def embed_kernel(
    n_rows, n_cents, emb_hbm, deg_hbm, rotation_hbm, offset_hbm, seed_hbm, energy_ref, center_ref,
    held, degree, rotation, offset, seeds, pick, scores, probs, across, mine, theirs,
    load_sem, near_send, near_recv, side_send, side_recv, mate_send, mate_recv, send_sem, recv_sem,
):
    group, row, me = lax.axis_index("groups"), lax.axis_index("rows"), lax.axis_index("cents")
    local, width = emb_hbm.shape
    members = n_rows * n_cents
    total_rows = members * local
    count = center_ref.shape[0]
    half = n_rows // 2
    chunk = 128

    loads = [
        pltpu.make_async_copy(source, target, load_sem.at[index])
        for index, (source, target) in enumerate(
            (
                (emb_hbm, held.at[row * n_cents + me, pl.ds(0, local)]),
                (deg_hbm, degree),
                (seed_hbm, seeds),
                (rotation_hbm, rotation),
                (offset_hbm, offset),
            )
        )
    ]
    for load in loads:
        load.start()

    def cent(step):
        return lax.rem(me + step + n_cents, n_cents)

    def side(step):
        return lax.rem(row + 2 * step + n_rows, n_rows)

    mate = row + 1 - 2 * lax.rem(row, 2)
    barrier = pltpu.get_barrier_semaphore()
    peers = [(group, row, cent(step)) for step in range(1, n_cents)]
    peers += [(group, side(step), me) for step in range(1, half)] + [(group, mate, me)]
    for device in peers:
        pl.semaphore_signal(barrier, inc=1, device_id=device, device_id_type=MESH)

    def fill(first, last):
        for at in range(first, last, chunk):
            ids = lax.broadcasted_iota(jnp.int32, (chunk, count), 0) + at
            pick[at : at + chunk, :] = jnp.where(ids == seeds[...], 1.0, 0.0).astype(jnp.bfloat16)

    def pushed(slot, send, recv, device):
        return pltpu.make_async_remote_copy(
            src_ref=held.at[slot],
            dst_ref=held.at[slot],
            send_sem=send,
            recv_sem=recv,
            device_id=device,
            device_id_type=MESH,
        )

    loads[1].wait()
    tag = jnp.concatenate(
        [degree[...].astype(jnp.float32), jnp.zeros((1, width - local), jnp.float32)], axis=1
    )
    held[row * n_cents + me, local:, :] = jnp.broadcast_to(tag, (16, width)).astype(jnp.bfloat16)
    loads[0].wait()
    pl.semaphore_wait(barrier, len(peers))
    near = [
        pushed(row * n_cents + me, near_send.at[step - 1], near_recv.at[step - 1], (group, row, cent(step)))
        for step in range(1, n_cents)
    ]
    for copy in near:
        copy.start()
    sides, mates = [], []

    def to_side(step):
        for other in range(1, half):
            place = (other - 1) * n_cents + step
            copy = pushed(
                row * n_cents + cent(-step), side_send.at[place], side_recv.at[place], (group, side(other), me)
            )
            copy.start()
            sides.append(copy)

    def to_mate(other, step):
        place = other * n_cents + step
        copy = pushed(
            side(-other) * n_cents + cent(-step), mate_send.at[place], mate_recv.at[place], (group, mate, me)
        )
        copy.start()
        mates.append(copy)

    to_side(0)
    to_mate(0, 0)
    loads[2].wait()
    fill(0, total_rows // 2)
    for step in range(1, n_cents):
        near[step - 1].wait_recv()
        to_side(step)
        to_mate(0, step)
    fill(total_rows // 2, total_rows)
    for step in range(n_cents):
        for other in range(1, half):
            sides[step * (half - 1) + other - 1].wait_recv()
            to_mate(other, step)
    for copy in mates:
        copy.wait_recv()
    for copy in near + sides + mates:
        copy.wait_send()

    rows = held[:, :local, :].reshape(total_rows, width)
    gram = lax.dot_general(rows, rows, (((0,), (0,)), ((), ())), preferred_element_type=jnp.float32)
    eye = lax.broadcasted_iota(jnp.int32, gram.shape, 0) == lax.broadcasted_iota(jnp.int32, gram.shape, 1)
    shifted = gram / total_rows + jnp.where(eye, ridge, 0.0)
    tags = held[:, local:, :].astype(jnp.float32)
    weight = jnp.sqrt(jnp.concatenate([tags[index, :1, :local] for index in range(members)], axis=1))
    loads[3].wait()
    turned = lax.dot_general(
        inverse_factor(shifted),
        rotation[...],
        (((0,), (0,)), ((), ())),
        preferred_element_type=jnp.float32,
        precision=lax.Precision.HIGHEST,
    ).astype(jnp.bfloat16)

    mixed = jnp.dot(rows, turned, preferred_element_type=jnp.float32)
    length = jnp.sum(mixed * mixed, axis=1, keepdims=True)
    unit = (mixed * lax.rsqrt(length + 1e-06)).astype(jnp.bfloat16)
    turned_unit = unit.astype(jnp.float32).T
    norm = jnp.sum(turned_unit * turned_unit, axis=0, keepdims=True)
    across[...] = turned_unit.astype(jnp.bfloat16)
    picked = jnp.dot(across[...], pick[...], preferred_element_type=jnp.float32)
    loads[4].wait()
    center_ref[...] = picked.T + offset[...]

    scale = LOG2E / sharpness_scale
    for turn in range(ITERS):
        peak8 = jnp.full((8, total_rows), -jnp.inf, jnp.float32)
        for at in range(0, count, chunk):
            center = center_ref[at : at + chunk, :]
            square = jnp.sum(center * center, axis=1, keepdims=True) * scale
            dots = jnp.dot(center.astype(jnp.bfloat16), across[...], preferred_element_type=jnp.float32)
            score = dots * (2.0 * scale) - square
            scores[at : at + chunk, :] = score
            peak8 = jnp.maximum(peak8, jnp.max(score.reshape(chunk // 8, 8, total_rows), axis=0))
        peak = jnp.max(peak8, axis=0, keepdims=True)
        total8 = jnp.zeros((8, total_rows), jnp.float32)
        for at in range(0, count, chunk):
            prob = jnp.exp2(scores[at : at + chunk, :] - peak)
            probs[at : at + chunk, :] = prob.astype(jnp.bfloat16)
            total8 = total8 + jnp.sum(prob.reshape(chunk // 8, 8, total_rows), axis=0)
        total = jnp.sum(total8, axis=0, keepdims=True)
        mine[turn, 0:1, :] = peak
        mine[turn, 1:2, :] = total
        copies = []
        for step in range(1, n_cents):
            copy = pltpu.make_async_remote_copy(
                src_ref=mine.at[turn],
                dst_ref=theirs.at[turn, step - 1],
                send_sem=send_sem.at[turn, step - 1],
                recv_sem=recv_sem.at[turn, step - 1],
                device_id=(group, row, cent(step)),
                device_id_type=MESH,
            )
            copy.start()
            copies.append(copy)
        for copy in copies:
            copy.wait()
        top = peak
        for step in range(1, n_cents):
            top = jnp.maximum(top, theirs[turn, step - 1, 0:1, :])
        own = jnp.exp2(peak - top)
        whole = total * own
        for step in range(1, n_cents):
            whole = whole + theirs[turn, step - 1, 1:2, :] * jnp.exp2(theirs[turn, step - 1, 0:1, :] - top)
        share = weight * own / whole
        high = share.astype(jnp.bfloat16).astype(jnp.float32)
        sub = lax.broadcasted_iota(jnp.int32, (16, total_rows), 0)
        tail = jnp.where(sub == 0, high, jnp.where(sub == 1, share - high, 0.0)).astype(jnp.bfloat16)
        moved = jnp.concatenate(
            [
                (across[...].astype(jnp.float32) * share).astype(jnp.bfloat16),
                tail,
                jnp.zeros((width - 16, total_rows), jnp.bfloat16),
            ],
            axis=0,
        )
        for at in range(0, count, 256):
            sums = lax.dot_general(
                probs[at : at + 256, :], moved, (((1,), (1,)), ((), ())), preferred_element_type=jnp.float32
            )
            mass = sums[:, width : width + 1] + sums[:, width + 1 : width + 2]
            center_ref[at : at + 256, :] = (sums[:, :width] + center_ref[at : at + 256, :]) / (mass + 1.0)
        if turn == ITERS - 1:
            energy = top * LN2 + jnp.log(whole) - norm / sharpness_scale
            index = row * n_cents + me
            kept = jnp.zeros((1, local), jnp.float32)
            for place in range(members):
                kept = jnp.where(index == place, energy[:, place * local : (place + 1) * local], kept)
            energy_ref[...] = kept


def fits(n_rows, n_cents, local, width, count):
    total_rows = n_rows * n_cents * local
    return (
        n_rows % 2 == 0
        and n_cents > 1
        and width == 128
        and local <= width
        and local % 16 == 0
        and count % 256 == 0
        and total_rows % 256 == 0
        and total_rows * count <= 2 * 1024 * 1024
    )


def gathered_shards(n_rows, n_cents, embedding, degrees, rotation, offsets, seed_ids):
    local, width = embedding.shape
    members = n_rows * n_cents
    total_rows = local * members
    count = offsets.shape[0]
    half = n_rows // 2
    sides = max(half - 1, 1) * n_cents
    dma = pltpu.SemaphoreType.DMA
    energy, centers = pl.pallas_call(
        functools.partial(embed_kernel, n_rows, n_cents),
        out_shape=(
            jax.ShapeDtypeStruct((1, local), jnp.float32),
            jax.ShapeDtypeStruct((count, width), jnp.float32),
        ),
        in_specs=[pl.BlockSpec(memory_space=pl.ANY)] * 5,
        out_specs=(pl.BlockSpec(memory_space=pltpu.VMEM),) * 2,
        scratch_shapes=[
            pltpu.VMEM((members, local + 16, width), jnp.bfloat16),
            pltpu.VMEM((1, local), jnp.int32),
            pltpu.VMEM((width, width), jnp.float32),
            pltpu.VMEM((count, width), jnp.float32),
            pltpu.VMEM((1, count), jnp.int32),
            pltpu.VMEM((total_rows, count), jnp.bfloat16),
            pltpu.VMEM((count, total_rows), jnp.float32),
            pltpu.VMEM((count, total_rows), jnp.bfloat16),
            pltpu.VMEM((width, total_rows), jnp.bfloat16),
            pltpu.VMEM((ITERS, 2, total_rows), jnp.float32),
            pltpu.VMEM((ITERS, n_cents - 1, 2, total_rows), jnp.float32),
            dma((5,)),
            dma((n_cents - 1,)),
            dma((n_cents - 1,)),
            dma((sides,)),
            dma((sides,)),
            dma((half * n_cents,)),
            dma((half * n_cents,)),
            dma((ITERS, n_cents - 1)),
            dma((ITERS, n_cents - 1)),
        ],
        compiler_params=pltpu.CompilerParams(
            collective_id=0, has_side_effects=True, vmem_limit_bytes=VMEM_LIMIT
        ),
    )(embedding, degrees.reshape(1, local), rotation, offsets, seed_ids.reshape(1, count))
    return energy.reshape(local), centers


def solution(mesh):
    n_rows, n_cents = mesh.shape["rows"], mesh.shape["cents"]

    def program(embedding, degrees, rotation, offsets, seed_ids):
        if fits(n_rows, n_cents, *embedding.shape, offsets.shape[0]):
            return gathered_shards(n_rows, n_cents, embedding, degrees, rotation, offsets, seed_ids)
        return shards(embedding, degrees, rotation, offsets, seed_ids)

    placed = (
        P(("groups", "rows", "cents"), None),
        P(("groups", "rows", "cents")),
        P(),
        P(("groups", "cents"), None),
        P(("groups", "cents")),
    )
    return jax.shard_map(
        program,
        mesh=mesh,
        in_specs=placed,
        out_specs=(P(("groups", "rows", "cents")), P(("groups", "cents"), None)),
        check_vma=False,
    )
```

```python
import functools
import math

import jax
import jax.numpy as jnp
from jax import lax
from jax.experimental import pallas as pl
from jax.experimental.pallas import tpu as pltpu
from jax.sharding import PartitionSpec as P

ITERS = 2


sharpness_scale = 0.1
ridge = 0.01


def lower_factor(matrix):
    width = matrix.shape[0]
    positions = jnp.arange(width, dtype=jnp.int32)

    def column_step(index, factor):
        row_here = lax.dynamic_index_in_dim(factor, index, 0, keepdims=False)
        column = lax.dynamic_index_in_dim(matrix, index, 1, keepdims=False)
        column = column - jnp.dot(factor, row_here, precision=lax.Precision.HIGHEST)
        pivot = jnp.sqrt(lax.dynamic_index_in_dim(column, index, 0, keepdims=False))
        column = jnp.where(positions > index, column / pivot, jnp.zeros((), column.dtype))
        column = jnp.where(positions == index, pivot, column)
        return lax.dynamic_update_slice_in_dim(factor, column[:, None], index, 1)

    return lax.fori_loop(0, width, column_step, jnp.zeros(matrix.shape, matrix.dtype))


def upper_solve(factor, target):
    width = factor.shape[0]

    def row_step(count, solved):
        index = width - 1 - count
        column = lax.dynamic_index_in_dim(factor, index, 1, keepdims=False)
        pivot = lax.dynamic_index_in_dim(column, index, 0, keepdims=False)
        target_row = lax.dynamic_index_in_dim(target, index, 0, keepdims=False)
        value = (target_row - jnp.dot(column, solved, precision=lax.Precision.HIGHEST)) / pivot
        return lax.dynamic_update_slice_in_dim(solved, value[None, :], index, 0)

    return lax.fori_loop(0, width, row_step, jnp.zeros(target.shape, target.dtype))


def block_affinity_logits(rows_block, piece_entry_lengths, cent_bf, mean_point_sqlength):
    pairwise_dots = lax.dot_general(
        rows_block, cent_bf, (((1,), (1,)), ((), ())), preferred_element_type=jnp.float32
    )
    return (
        2.0 * pairwise_dots - mean_point_sqlength[None, :] - piece_entry_lengths[:, None]
    ) / sharpness_scale


def shards(embedding, degrees, rotation, offsets, seed_ids):
    local_entries = embedding.shape[0]
    width = embedding.shape[1]
    total_rows = local_entries * lax.axis_size("rows") * lax.axis_size("cents")
    partial_gram_matrix = lax.dot_general(
        embedding, embedding, (((0,), (0,)), ((), ())), preferred_element_type=jnp.float32
    )
    gram = lax.psum(partial_gram_matrix, ("rows", "cents"))
    shifted = gram / total_rows + ridge * jnp.eye(width, dtype=jnp.float32)
    cholesky_lower_factor = lower_factor(shifted)
    turned = upper_solve(cholesky_lower_factor, rotation).astype(jnp.bfloat16)
    mixed = jnp.dot(embedding, turned, preferred_element_type=jnp.float32)
    unit = (mixed * lax.rsqrt(jnp.sum(mixed * mixed, axis=1, keepdims=True) + 1e-06)).astype(
        jnp.bfloat16
    )
    gathered, degree_rows = (
        lax.all_gather(unit, "cents", axis=0, tiled=True),
        lax.all_gather(degrees.astype(jnp.bfloat16), "cents", axis=0, tiled=True),
    )
    count = gathered.shape[0]
    weights = jnp.sqrt(degree_rows.astype(jnp.float32))
    sq_norms = jnp.sum(jnp.square(gathered.astype(jnp.float32)), axis=1)
    local_ids = seed_ids - lax.axis_index("rows") * count
    block_rows = min(512, count)
    block_count = count // block_rows
    rows_blocks = gathered.reshape(block_count, block_rows, width)
    norm_blocks = sq_norms.reshape(block_count, block_rows)
    weight_blocks = weights.reshape(block_count, block_rows)
    block_starts = jnp.arange(block_count, dtype=jnp.int32) * block_rows
    row_positions = jnp.arange(block_rows, dtype=jnp.int32)

    def seed_block(carry, pack):
        selector = ((local_ids - pack[1])[:, None] == row_positions[None, :]).astype(jnp.bfloat16)
        return (carry + jnp.dot(selector, pack[0], preferred_element_type=jnp.float32), None)

    picked_sum, unused_seed = lax.scan(
        seed_block, jnp.zeros((seed_ids.shape[0], width), jnp.float32), (rows_blocks, block_starts)
    )
    picked = picked_sum.astype(jnp.bfloat16)
    centers = lax.psum(picked, "rows").astype(jnp.float32) + offsets
    energy = jnp.zeros((count,), jnp.float32)
    for step in range(ITERS):
        cent_bf = centers.astype(jnp.bfloat16)
        mean_point_sqlength = jnp.sum(centers * centers, axis=1)

        def local_stats(pack):
            logits = block_affinity_logits(pack[0], pack[1], cent_bf, mean_point_sqlength)
            peak = jnp.max(logits, axis=1)
            return (peak, jnp.sum(jnp.exp(logits - peak[:, None]), axis=1))

        peaks, totals = lax.map(local_stats, (rows_blocks, norm_blocks))
        larger = lax.pmax(peaks, "cents")
        whole = lax.psum(totals * jnp.exp(peaks - larger), "cents")

        def accumulate(carry, pack):
            logits = block_affinity_logits(pack[0], pack[1], cent_bf, mean_point_sqlength)
            probs = jnp.exp(logits - pack[2][:, None]) / pack[3][:, None]
            shares = (pack[4][:, None] * probs).astype(jnp.bfloat16)
            moved = lax.dot_general(
                shares, pack[0], (((0,), (0,)), ((), ())), preferred_element_type=jnp.float32
            )
            return (
                (carry[0] + moved, carry[1] + jnp.sum(shares.astype(jnp.float32), axis=0)),
                None,
            )

        start = (jnp.zeros(centers.shape, jnp.float32), jnp.zeros((centers.shape[0],), jnp.float32))
        (sums, masses), unused = lax.scan(
            accumulate, start, (rows_blocks, norm_blocks, larger, whole, weight_blocks)
        )
        energy = (larger + jnp.log(whole)).reshape(count)
        full_sums, full_masses = (
            lax.psum(sums.astype(jnp.bfloat16), "rows").astype(jnp.float32),
            lax.psum(masses.astype(jnp.bfloat16), "rows").astype(jnp.float32),
        )
        centers = (full_sums + centers) / (full_masses + 1.0)[:, None]
    own_energy = lax.dynamic_slice_in_dim(
        energy, lax.axis_index("cents") * local_entries, local_entries
    )
    return (own_energy, centers)


MESH = pl.DeviceIdType.MESH
LOG2E = math.log2(math.e)
LN2 = math.log(2.0)
VMEM_LIMIT = 56 * 1024 * 1024
BLOCK = 32


def inverse_factor(matrix):
    width = matrix.shape[0]
    row_id = lax.broadcasted_iota(jnp.int32, (width, width), 0)
    col_id = lax.broadcasted_iota(jnp.int32, (width, width), 1)
    left = matrix
    right = jnp.where(row_id == col_id, 1.0, 0.0).astype(jnp.float32)
    sub = lax.broadcasted_iota(jnp.int32, (BLOCK, width), 0)
    solved = []
    for at in range(0, width, BLOCK):
        a, v = left[:BLOCK], right[:BLOCK]
        columns = [jnp.broadcast_to(a[:, at + j : at + j + 1], (BLOCK, width)) for j in range(BLOCK)]
        pivots = jnp.ones((BLOCK, width), jnp.float32)
        for j in range(BLOCK):
            low = j // 8 * 8

            def lower(old, new):
                return new if low == 0 else jnp.concatenate([old[:low], new], axis=0)

            pivot = columns[j][j : j + 1, :]
            pivots = jnp.where(sub == j, pivot, pivots)
            share = jnp.where(sub[low:] > j, columns[j][low:] * (1.0 / pivot), 0.0)
            for l in range(j + 1, BLOCK):
                columns[l] = lower(columns[l], columns[l][low:] - share * columns[l][j : j + 1, :])
            a = lower(a, a[low:] - share * a[j : j + 1, :])
            v = lower(v, v[low:] - share * v[j : j + 1, :])
        solved.append(v * lax.rsqrt(pivots))
        if at + BLOCK < width:
            update = lax.dot_general(
                a / pivots,
                jnp.concatenate([a, v], axis=1),
                (((0,), (0,)), ((), ())),
                preferred_element_type=jnp.float32,
                precision=lax.Precision.HIGHEST,
            )[at + BLOCK :]
            left = left[BLOCK:] - update[:, :width]
            right = right[BLOCK:] - update[:, width:]
    return jnp.concatenate(solved, axis=0)


def embed_kernel(
    n_rows, n_cents, emb_hbm, deg_hbm, rotation_hbm, offset_hbm, seed_hbm, energy_ref, center_ref,
    held, degree, rotation, offset, seeds, pick, scores, probs, across, mine, theirs,
    load_sem, near_send, near_recv, mate_send, mate_recv, send_sem, recv_sem,
):
    group, row, me = lax.axis_index("groups"), lax.axis_index("rows"), lax.axis_index("cents")
    local, width = emb_hbm.shape
    members = n_rows * n_cents
    total_rows = members * local
    count = center_ref.shape[0]
    half = n_rows // 2
    chunk = 128

    loads = [
        pltpu.make_async_copy(source, target, load_sem.at[index])
        for index, (source, target) in enumerate(
            (
                (emb_hbm, held.at[row * n_cents + me, pl.ds(0, local)]),
                (deg_hbm, degree),
                (seed_hbm, seeds),
                (rotation_hbm, rotation),
                (offset_hbm, offset),
            )
        )
    ]
    for load in loads:
        load.start()

    def cent(step):
        return lax.rem(me + step + n_cents, n_cents)

    def side(step):
        return lax.rem(row + 2 * step + n_rows, n_rows)

    mate = row + 1 - 2 * lax.rem(row, 2)
    barrier = pltpu.get_barrier_semaphore()
    far = [(other, step) for step in range(n_cents) for other in range(half)][1:]
    peers = [(group, side(other), cent(step)) for other, step in far] + [(group, mate, me)]
    for device in peers:
        pl.semaphore_signal(barrier, inc=1, device_id=device, device_id_type=MESH)

    def fill(first, last):
        for at in range(first, last, chunk):
            ids = lax.broadcasted_iota(jnp.int32, (chunk, count), 0) + at
            pick[at : at + chunk, :] = jnp.where(ids == seeds[...], 1.0, 0.0).astype(jnp.bfloat16)

    def pushed(slot, send, recv, device):
        return pltpu.make_async_remote_copy(
            src_ref=held.at[slot],
            dst_ref=held.at[slot],
            send_sem=send,
            recv_sem=recv,
            device_id=device,
            device_id_type=MESH,
        )

    loads[1].wait()
    tag = jnp.concatenate(
        [degree[...].astype(jnp.float32), jnp.zeros((1, width - local), jnp.float32)], axis=1
    )
    held[row * n_cents + me, local:, :] = jnp.broadcast_to(tag, (16, width)).astype(jnp.bfloat16)
    loads[0].wait()
    loads[2].wait()
    fill(0, total_rows)
    pl.semaphore_wait(barrier, len(peers))
    near, mates = [], []
    for place, (other, step) in enumerate(far):
        copy = pushed(
            row * n_cents + me, near_send.at[place], near_recv.at[place], (group, side(other), cent(step))
        )
        copy.start()
        near.append(copy)
    for place, (other, step) in enumerate([(0, 0)] + far):
        if place:
            near[place - 1].wait_recv()
        copy = pushed(
            side(-other) * n_cents + cent(-step), mate_send.at[place], mate_recv.at[place], (group, mate, me)
        )
        copy.start()
        mates.append(copy)
    for copy in mates:
        copy.wait_recv()
    for copy in near + mates:
        copy.wait_send()

    rows = held[:, :local, :].reshape(total_rows, width)
    gram = lax.dot_general(rows, rows, (((0,), (0,)), ((), ())), preferred_element_type=jnp.float32)
    eye = lax.broadcasted_iota(jnp.int32, gram.shape, 0) == lax.broadcasted_iota(jnp.int32, gram.shape, 1)
    shifted = gram / total_rows + jnp.where(eye, ridge, 0.0)
    tags = held[:, local:, :].astype(jnp.float32)
    weight = jnp.sqrt(jnp.concatenate([tags[index, :1, :local] for index in range(members)], axis=1))
    loads[3].wait()
    turned = lax.dot_general(
        inverse_factor(shifted),
        rotation[...],
        (((0,), (0,)), ((), ())),
        preferred_element_type=jnp.float32,
        precision=lax.Precision.HIGHEST,
    ).astype(jnp.bfloat16)

    mixed = jnp.dot(rows, turned, preferred_element_type=jnp.float32)
    length = jnp.sum(mixed * mixed, axis=1, keepdims=True)
    unit = (mixed * lax.rsqrt(length + 1e-06)).astype(jnp.bfloat16)
    turned_unit = unit.astype(jnp.float32).T
    norm = jnp.sum(turned_unit * turned_unit, axis=0, keepdims=True)
    across[...] = turned_unit.astype(jnp.bfloat16)
    picked = jnp.dot(across[...], pick[...], preferred_element_type=jnp.float32)
    loads[4].wait()
    center_ref[...] = picked.T + offset[...]

    scale = LOG2E / sharpness_scale
    for turn in range(ITERS):
        peak8 = jnp.full((8, total_rows), -jnp.inf, jnp.float32)
        for at in range(0, count, chunk):
            center = center_ref[at : at + chunk, :]
            square = jnp.sum(center * center, axis=1, keepdims=True) * scale
            dots = jnp.dot(center.astype(jnp.bfloat16), across[...], preferred_element_type=jnp.float32)
            score = dots * (2.0 * scale) - square
            scores[at : at + chunk, :] = score
            peak8 = jnp.maximum(peak8, jnp.max(score.reshape(chunk // 8, 8, total_rows), axis=0))
        peak = jnp.max(peak8, axis=0, keepdims=True)
        total8 = jnp.zeros((8, total_rows), jnp.float32)
        for at in range(0, count, chunk):
            prob = jnp.exp2(scores[at : at + chunk, :] - peak)
            probs[at : at + chunk, :] = prob.astype(jnp.bfloat16)
            total8 = total8 + jnp.sum(prob.reshape(chunk // 8, 8, total_rows), axis=0)
        total = jnp.sum(total8, axis=0, keepdims=True)
        mine[turn, 0:1, :] = peak
        mine[turn, 1:2, :] = total
        copies = []
        for step in range(1, n_cents):
            copy = pltpu.make_async_remote_copy(
                src_ref=mine.at[turn],
                dst_ref=theirs.at[turn, step - 1],
                send_sem=send_sem.at[turn, step - 1],
                recv_sem=recv_sem.at[turn, step - 1],
                device_id=(group, row, cent(step)),
                device_id_type=MESH,
            )
            copy.start()
            copies.append(copy)
        for copy in copies:
            copy.wait()
        top = peak
        for step in range(1, n_cents):
            top = jnp.maximum(top, theirs[turn, step - 1, 0:1, :])
        own = jnp.exp2(peak - top)
        whole = total * own
        for step in range(1, n_cents):
            whole = whole + theirs[turn, step - 1, 1:2, :] * jnp.exp2(theirs[turn, step - 1, 0:1, :] - top)
        share = weight * own / whole
        high = share.astype(jnp.bfloat16).astype(jnp.float32)
        sub = lax.broadcasted_iota(jnp.int32, (16, total_rows), 0)
        tail = jnp.where(sub == 0, high, jnp.where(sub == 1, share - high, 0.0)).astype(jnp.bfloat16)
        moved = jnp.concatenate(
            [
                (across[...].astype(jnp.float32) * share).astype(jnp.bfloat16),
                tail,
                jnp.zeros((width - 16, total_rows), jnp.bfloat16),
            ],
            axis=0,
        )
        for at in range(0, count, 256):
            sums = lax.dot_general(
                probs[at : at + 256, :], moved, (((1,), (1,)), ((), ())), preferred_element_type=jnp.float32
            )
            mass = sums[:, width : width + 1] + sums[:, width + 1 : width + 2]
            center_ref[at : at + 256, :] = (sums[:, :width] + center_ref[at : at + 256, :]) / (mass + 1.0)
        if turn == ITERS - 1:
            energy = top * LN2 + jnp.log(whole) - norm / sharpness_scale
            index = row * n_cents + me
            kept = jnp.zeros((1, local), jnp.float32)
            for place in range(members):
                kept = jnp.where(index == place, energy[:, place * local : (place + 1) * local], kept)
            energy_ref[...] = kept


def finish_kernel(energy_in, center_in, energy_out, center_out):
    energy_out[...] = energy_in[...]
    center_out[...] = center_in[...]


def fits(n_rows, n_cents, local, width, count):
    total_rows = n_rows * n_cents * local
    return (
        n_rows % 2 == 0
        and n_cents > 1
        and width == 128
        and local <= width
        and local % 16 == 0
        and count % 256 == 0
        and total_rows % 256 == 0
        and total_rows * count <= 2 * 1024 * 1024
    )


def gathered_shards(n_rows, n_cents, embedding, degrees, rotation, offsets, seed_ids):
    local, width = embedding.shape
    members = n_rows * n_cents
    total_rows = local * members
    count = offsets.shape[0]
    half = n_rows // 2
    dma = pltpu.SemaphoreType.DMA
    energy, centers = pl.pallas_call(
        functools.partial(embed_kernel, n_rows, n_cents),
        out_shape=(
            jax.ShapeDtypeStruct((1, local), jnp.float32),
            jax.ShapeDtypeStruct((count, width), jnp.float32),
        ),
        in_specs=[pl.BlockSpec(memory_space=pl.ANY)] * 5,
        out_specs=(pl.BlockSpec(memory_space=pltpu.VMEM),) * 2,
        scratch_shapes=[
            pltpu.VMEM((members, local + 16, width), jnp.bfloat16),
            pltpu.VMEM((1, local), jnp.int32),
            pltpu.VMEM((width, width), jnp.float32),
            pltpu.VMEM((count, width), jnp.float32),
            pltpu.VMEM((1, count), jnp.int32),
            pltpu.VMEM((total_rows, count), jnp.bfloat16),
            pltpu.VMEM((count, total_rows), jnp.float32),
            pltpu.VMEM((count, total_rows), jnp.bfloat16),
            pltpu.VMEM((width, total_rows), jnp.bfloat16),
            pltpu.VMEM((ITERS, 2, total_rows), jnp.float32),
            pltpu.VMEM((ITERS, n_cents - 1, 2, total_rows), jnp.float32),
            dma((5,)),
            dma((half * n_cents - 1,)),
            dma((half * n_cents - 1,)),
            dma((half * n_cents,)),
            dma((half * n_cents,)),
            dma((ITERS, n_cents - 1)),
            dma((ITERS, n_cents - 1)),
        ],
        compiler_params=pltpu.CompilerParams(
            collective_id=0, has_side_effects=True, vmem_limit_bytes=VMEM_LIMIT
        ),
    )(embedding, degrees.reshape(1, local), rotation, offsets, seed_ids.reshape(1, count))
    energy, centers = pl.pallas_call(
        finish_kernel,
        out_shape=(
            jax.ShapeDtypeStruct((1, local), jnp.float32),
            jax.ShapeDtypeStruct((count, width), jnp.float32),
        ),
        in_specs=[pl.BlockSpec(memory_space=pltpu.VMEM)] * 2,
        out_specs=(pl.BlockSpec(memory_space=pltpu.VMEM),) * 2,
    )(energy, centers)
    return energy.reshape(local), centers


def solution(mesh):
    n_rows, n_cents = mesh.shape["rows"], mesh.shape["cents"]

    def program(embedding, degrees, rotation, offsets, seed_ids):
        if fits(n_rows, n_cents, *embedding.shape, offsets.shape[0]):
            return gathered_shards(n_rows, n_cents, embedding, degrees, rotation, offsets, seed_ids)
        return shards(embedding, degrees, rotation, offsets, seed_ids)

    placed = (
        P(("groups", "rows", "cents"), None),
        P(("groups", "rows", "cents")),
        P(),
        P(("groups", "cents"), None),
        P(("groups", "cents")),
    )
    return jax.shard_map(
        program,
        mesh=mesh,
        in_specs=placed,
        out_specs=(P(("groups", "rows", "cents")), P(("groups", "cents"), None)),
        check_vma=False,
    )
```
